32 devices in a mesh: tm: 8 (over z, x), head: 4 (over y, core).
Axes of the slice: x: 2, y: 2, z: 4, core: 2. Of those that a mesh axis runs over, the one named last changes fastest.
Arguments:
- latents: bfloat16 [6144, 3072], P('tm', 'head'), may hold values from -6 to 6
- w_query: bfloat16 [3072, 1536], P(None, 'head'), may hold values from -0.109375 to 0.109375
- w_key: bfloat16 [3072, 1536], P(None, 'head'), may hold values from -0.109375 to 0.109375
- w_value: bfloat16 [3072, 1536], P(None, 'head'), may hold values from -0.109375 to 0.109375
- q_gain: float32 [128], replicated, may hold values from 1 to 2
- k_gain: float32 [128], replicated, may hold values from 1 to 2
- w_out: bfloat16 [1536, 3072], P('head'), may hold values from -0.15625 to 0.15625
- neighbours: int32 [16, 4], P('tm'), may hold values from 0 to 15, as said below
- tile_slot: int32 [16], replicated, may hold values from 0 to 15, as said below
- slab_dest: int32 [8], replicated, may hold values from 0 to 7, as said below
Outputs:
- handed: bfloat16 [6144, 3072], P('tm', 'head')
The draws below stay inside these ranges and needn't reach their ends.
Inputs may be any that keep to these rules, and one draw needn't show every extreme that they name: `neighbours`: entry 0 of row g is g; the other 3 entries of a row are distinct tiles other than g from the slabs g // 2 - 1, g // 2 and g // 2 + 1 that exist. A permutation that keeps every tile in its own slab: tile_slot[g] // 2 == g // 2. slab_dest[s] = (s + r) % 8 for one r of 1 to 7.
All inputs are finite; a program needn't handle non-finite values.
Results may differ from the reference program's by a relative error of at most 0.012.
Values may be sent and summed in bfloat16 or wider, within the bound.
No kernel may reach another device: no remote copies, remote signals or barrier semaphores. Data moves between devices by JAX's collectives and lax.ppermute only.
A program may use at most 128 MiB of HBM per device.

```python
import math
import jax
import jax.numpy as jnp
from jax import lax

D = 3072
HEADS = 12
HEAD_DIM = 128
TILE = 384
NB = 4
TILE_DEV = 2
TILES = 16
TOKENS = 6144
N_TM = 8
N_HEAD = 4


def draw_neighbours(key, part):
    own_tiles = jnp.arange(TILES, dtype=jnp.int32)
    slab_index = own_tiles // TILE_DEV
    offsets = jnp.arange(3 * TILE_DEV, dtype=jnp.int32)
    candidates = (slab_index[:, None] - 1) * TILE_DEV + offsets[None, :]
    usable = (candidates >= 0) & (candidates < TILES) & (candidates != own_tiles[:, None])
    noise_bits = jax.random.randint(key, (TILES, 3 * TILE_DEV), 0, 1 << 20, dtype=jnp.int32)
    ranking = jnp.where(usable, noise_bits * (3 * TILE_DEV) + offsets[None, :], -1)
    _, chosen = lax.top_k(ranking, NB - 1)
    others = jnp.take_along_axis(candidates, chosen, axis=1)
    return jnp.concatenate([own_tiles[:, None], others], axis=1).astype(jnp.int32)


def draw_tile_slot(key, part):
    slab_count = TILES // TILE_DEV
    offsets = jnp.arange(TILE_DEV, dtype=jnp.int32)
    noise_bits = jax.random.randint(key, (slab_count, TILE_DEV), 0, 1 << 20, dtype=jnp.int32) * TILE_DEV + offsets[None, :]
    ordering = jnp.argsort(noise_bits, axis=1, stable=True).astype(jnp.int32)
    placed = jnp.arange(slab_count, dtype=jnp.int32)[:, None] * TILE_DEV + ordering
    return placed.reshape(TILES).astype(jnp.int32)


def draw_slab_dest(key, part):
    slab_count = TILES // TILE_DEV
    rotation = jax.random.randint(key, (), 1, slab_count, dtype=jnp.int32)
    return ((jnp.arange(slab_count, dtype=jnp.int32) + rotation) % slab_count).astype(jnp.int32)


def block_levels(own_key, shape, split, low, top_value):
    def one(axis_at, shards_of):
        heights = jax.random.uniform(jax.random.fold_in(jax.random.fold_in(own_key, 6), axis_at), (shards_of,), jnp.float32, low / len(split), top_value / len(split))
        return jnp.repeat(jnp.exp(heights), shape[axis_at] // shards_of).reshape((-1,) + (1,) * (len(shape) - axis_at - 1))

    loudness = one(*split[0])
    for cut in split[1:]:
        loudness = loudness * one(*cut)
    return loudness


def gaussian(rng, shape, deviation, most, pieces=(), held_as=jnp.bfloat16):
    level = block_levels(rng, shape, pieces, -0.22, 0.18) if pieces else 1.0
    values = jax.random.normal(rng, shape, jnp.float32) * deviation * level
    return jnp.minimum(jnp.maximum(values, -most), most).astype(held_as)


def setup_inputs(seed: int = 0) -> dict:
    key_list = jax.random.split(jax.random.key(seed), 11)
    return {
        "latents": gaussian(key_list[0], (TOKENS, D), 1.0, 6.0, ((0, 8), (1, 4))),
        "w_query": gaussian(key_list[1], (D, HEADS * HEAD_DIM), D ** -0.5, 0.109375, ((1, 4),)),
        "w_key": gaussian(key_list[2], (D, HEADS * HEAD_DIM), D ** -0.5, 0.109375, ((1, 4),)),
        "w_value": gaussian(key_list[3], (D, HEADS * HEAD_DIM), D ** -0.5, 0.109375, ((1, 4),)),
        "q_gain": jnp.clip(jax.random.uniform(key_list[4], (HEAD_DIM,), jnp.float32, 1.0, 2.0), 1.0, 2.0),
        "k_gain": jnp.clip(jax.random.uniform(key_list[5], (HEAD_DIM,), jnp.float32, 1.0, 2.0), 1.0, 2.0),
        "w_out": gaussian(key_list[6], (HEADS * HEAD_DIM, D), (HEADS * HEAD_DIM) ** -0.5, 0.15625, ((0, 4),)),
        "neighbours": draw_neighbours(jax.random.fold_in(key_list[10], 71), 0),
        "tile_slot": draw_tile_slot(jax.random.fold_in(key_list[10], 71), 0),
        "slab_dest": draw_slab_dest(jax.random.fold_in(key_list[10], 71), 0),
    }


def normed(values_in, gain):
    mean_square = lax.optimization_barrier(jnp.mean(values_in * values_in, axis=-1, keepdims=True))
    return values_in * lax.rsqrt(mean_square + 1e-06) * gain

def reference(latents, w_query, w_key, w_value, q_gain, k_gain, w_out, neighbours, tile_slot, slab_dest):
    queries = normed(jnp.dot(latents, w_query, preferred_element_type=jnp.float32).reshape(TOKENS, HEADS, HEAD_DIM), q_gain).astype(jnp.bfloat16)
    keys_all = normed(jnp.dot(latents, w_key, preferred_element_type=jnp.float32).reshape(TOKENS, HEADS, HEAD_DIM), k_gain).astype(jnp.bfloat16)
    values_all = jnp.dot(latents, w_value, preferred_element_type=jnp.float32).astype(jnp.bfloat16).reshape(TOKENS, HEADS, HEAD_DIM)
    query_tiles = queries.reshape(TILES, TILE, HEADS, HEAD_DIM)
    key_tiles = keys_all.reshape(TILES, TILE, HEADS, HEAD_DIM)
    value_tiles = values_all.reshape(TILES, TILE, HEADS, HEAD_DIM)
    scaling = 1.0 / math.sqrt(HEAD_DIM)

    def one_tile(tile_index):
        home_block = tile_slot[tile_index]
        sources = jnp.take(tile_slot, neighbours[tile_index]).astype(jnp.int32)
        q_block = query_tiles[home_block].astype(jnp.float32)
        k_block = jnp.take(key_tiles, sources, axis=0).reshape(NB * TILE, HEADS, HEAD_DIM).astype(jnp.float32)
        v_block = jnp.take(value_tiles, sources, axis=0).reshape(NB * TILE, HEADS, HEAD_DIM).astype(jnp.float32)
        scores = jnp.einsum('qhd,khd->hqk', q_block, k_block) * scaling
        raised = jnp.exp(scores)
        probs = (raised / lax.optimization_barrier(jnp.sum(raised, axis=-1, keepdims=True))).astype(jnp.bfloat16)
        return jnp.einsum('hqk,khd->qhd', probs.astype(jnp.float32), v_block).astype(jnp.bfloat16)
    results = lax.map(one_tile, jnp.arange(TILES, dtype=jnp.int32))
    attention = jnp.zeros_like(query_tiles).at[tile_slot].set(results).reshape(TOKENS, HEADS * HEAD_DIM)
    group_width = HEADS * HEAD_DIM // N_HEAD
    total = jnp.zeros((TOKENS, D), jnp.float32)
    for group_index in range(N_HEAD):
        low = group_index * group_width
        partial_value = jnp.dot(attention[:, low:low + group_width], w_out[low:low + group_width], preferred_element_type=jnp.float32)
        partial_value = lax.optimization_barrier(partial_value.astype(jnp.bfloat16)).astype(jnp.float32)
        total = total + partial_value
    layer_out = total.astype(jnp.bfloat16)
    slabs = layer_out.reshape(N_TM, TILE_DEV * TILE, D)
    handed = jnp.zeros_like(slabs).at[slab_dest].set(slabs)
    return handed.reshape(TOKENS, D)
```

```python
import functools
import math

import jax
import jax.numpy as jnp
from jax import lax
from jax.experimental import pallas as pl
from jax.experimental.pallas import tpu as pltpu
from jax.sharding import PartitionSpec as P

HEAD_DIM = 128
RADIX = 8
EPS = 1e-6
VMEM = pltpu.MemorySpace.VMEM
SMEM = pltpu.MemorySpace.SMEM


def in_vmem(count):
    return [pl.BlockSpec(memory_space=VMEM)] * count


def in_smem(count):
    return [pl.BlockSpec(memory_space=SMEM)] * count


def params(mib):
    return pltpu.CompilerParams(vmem_limit_bytes=mib * 1024 * 1024)


def flipped(value, bits):
    count = lax.axis_size("head")
    return lax.ppermute(value, "head", [(i, i ^ bits) for i in range(count)])


def gathered(piece):
    have = {0: piece}
    bit = lax.axis_size("head") // 2
    while bit:
        for key in list(have):
            have[key | bit] = flipped(have[key], bit)
        bit //= 2
    return [have[key] for key in sorted(have)]


def exchanged(value):
    count = lax.axis_size("tm")
    return lax.ppermute(value, "tm", [(i, i ^ 1) for i in range(count)])


def relayed(value):
    count = lax.axis_size("tm")
    pairs = [(i, i - 2) for i in range(3, count, 2)]
    pairs += [(i, i + 2) for i in range(0, count - 2, 2)]
    return lax.ppermute(value, "tm", pairs)


def normed(sums, gain):
    mean_square = jnp.mean(sums * sums, axis=-1, keepdims=True)
    return sums * lax.rsqrt(mean_square + EPS) * gain


def project_body(parts, place, *refs):
    pieces = refs[:parts]
    w_query, w_key, w_value, q_gain, k_gain, q_out, kv_out = refs[parts:]
    me = place[1]
    depth = pieces[0].shape[1]
    cols = w_query.shape[1]

    def sums(weight):
        total = None
        for key in range(parts):
            rows = pl.ds(pl.multiple_of((me ^ key) * depth, depth), depth)
            term = jnp.dot(
                pieces[key][...], weight[rows, :], preferred_element_type=jnp.float32
            )
            total = term if total is None else total + term
        return total

    for weight, gain, out, base in (
        (w_query, q_gain, q_out, 0),
        (w_key, k_gain, kv_out, 0),
    ):
        raw = sums(weight)
        for low in range(0, cols, HEAD_DIM):
            head = normed(raw[:, low : low + HEAD_DIM], gain[...])
            out[:, base + low : base + low + HEAD_DIM] = head.astype(jnp.bfloat16)
    kv_out[:, cols:] = sums(w_value).astype(jnp.bfloat16)


def project(place, pieces, w_query, w_key, w_value, q_gain, k_gain):
    rows, depth = pieces[0].shape
    cols = w_query.shape[1]
    parts = len(pieces)
    flops = 2 * rows * depth * parts * cols * 3
    return pl.pallas_call(
        functools.partial(project_body, parts),
        out_shape=(
            jax.ShapeDtypeStruct((rows, cols), jnp.bfloat16),
            jax.ShapeDtypeStruct((rows, 2 * cols), jnp.bfloat16),
        ),
        in_specs=in_smem(1) + in_vmem(parts + 5),
        out_specs=tuple(in_vmem(2)),
        compiler_params=params(24),
        cost_estimate=pl.CostEstimate(
            flops=flops, bytes_accessed=3 * depth * parts * cols * 2, transcendentals=0
        ),
        name="project",
    )(place, *pieces, w_query, w_key, w_value, q_gain, k_gain)


def mark_chosen(place, neighbours, tile_slot, chosen):
    tiles, window = neighbours.shape
    slab = place[0]
    for i in range(3 * tiles * tiles):
        chosen[i] = 0
    for tile in range(tiles):
        home = tile_slot[slab * tiles + tile] - slab * tiles
        for j in range(window):
            source = tile_slot[neighbours[tile, j]] - (slab - 1) * tiles
            chosen[home * (3 * tiles) + source] = 1


def attend_body(tiles, pieces, groups, first, place, neighbours, tile_slot, *refs):
    q_refs = refs[: tiles * pieces]
    at = tiles * pieces
    slabs = []
    for _ in groups:
        slabs.append(refs[at : at + tiles * pieces])
        at += tiles * pieces
    if first:
        acc, part, q_buf, chosen = refs[at:]
    else:
        acc_in, part_in, *outs, q_buf, acc, part, chosen = refs[at:]
    mark_chosen(place, neighbours, tile_slot, chosen)
    length = sum(q_refs[i].shape[0] for i in range(pieces))
    cols = q_refs[0].shape[1]
    heads = cols // HEAD_DIM
    low = 0
    for ref in q_refs:
        q_buf[low : low + ref.shape[0], :] = ref[...]
        low += ref.shape[0]
    if first:
        acc[...] = jnp.zeros_like(acc)
        part[...] = jnp.zeros_like(part)
    else:
        acc[...] = acc_in[...]
        part[...] = part_in[...]
    odd = lax.rem(place[0], 2)
    bases = {"own": tiles, "partner": 2 * tiles * (1 - odd), "other": 2 * tiles * odd}
    scaling = 1.0 / math.sqrt(HEAD_DIM)

    def step(i, carry):
        block = i // heads
        head = lax.rem(i, heads)
        rows = pl.ds(pl.multiple_of(block * length, length), length)
        lanes = pl.ds(pl.multiple_of(head * HEAD_DIM, HEAD_DIM), HEAD_DIM)
        v_lanes = pl.ds(pl.multiple_of(cols + head * HEAD_DIM, HEAD_DIM), HEAD_DIM)
        for group, slab in zip(groups, slabs):
            for tile in range(tiles):
                own = slab[tile * pieces : (tile + 1) * pieces]

                @pl.when(chosen[block * (3 * tiles) + bases[group] + tile] > 0)
                def _():
                    keys = jnp.concatenate([ref[:, lanes] for ref in own], axis=0)
                    vals = jnp.concatenate([ref[:, v_lanes] for ref in own], axis=0)
                    scores = lax.dot_general(
                        q_buf[rows, lanes],
                        keys,
                        (((1,), (1,)), ((), ())),
                        preferred_element_type=jnp.float32,
                    )
                    raised = jnp.exp(scores * scaling)
                    wide = raised[:, :HEAD_DIM]
                    for at_lane in range(HEAD_DIM, length, HEAD_DIM):
                        wide = wide + raised[:, at_lane : at_lane + HEAD_DIM]
                    part[rows, lanes] += wide
                    acc[rows, lanes] += jnp.dot(
                        raised.astype(jnp.bfloat16), vals, preferred_element_type=jnp.float32
                    )

        return carry

    lax.fori_loop(0, tiles * heads, step, 0)
    if not first:
        for tile, out in enumerate(outs):
            rows = slice(tile * length, (tile + 1) * length)
            for lane in range(0, cols, HEAD_DIM):
                lanes = slice(lane, lane + HEAD_DIM)
                total = jnp.sum(part[rows, lanes], axis=-1, keepdims=True)
                out[:, lanes] = (acc[rows, lanes] / total).astype(jnp.bfloat16)


def attend(place, neighbours, tile_slot, queries, slabs, groups, state):
    tiles = neighbours.shape[0]
    pieces = len(queries) // tiles
    rows = sum(q.shape[0] for q in queries)
    cols = queries[0].shape[1]
    length = rows // tiles
    wide = jax.ShapeDtypeStruct((rows, cols), jnp.float32)
    first = state is None
    flat = [piece for slab in slabs for piece in slab]
    scratch = [pltpu.VMEM((rows, cols), jnp.bfloat16)]
    if first:
        outs = (wide, wide)
        extra = []
    else:
        outs = tuple(jax.ShapeDtypeStruct((length, cols), jnp.bfloat16) for _ in range(tiles))
        extra = list(state)
        scratch += [pltpu.VMEM((rows, cols), jnp.float32)] * 2
    scratch.append(pltpu.SMEM((3 * tiles * tiles,), jnp.int32))
    return pl.pallas_call(
        functools.partial(attend_body, tiles, pieces, groups, first),
        out_shape=outs,
        in_specs=in_smem(3) + in_vmem(len(queries) + len(flat) + len(extra)),
        out_specs=tuple(in_vmem(len(outs))),
        scratch_shapes=scratch,
        compiler_params=params(24),
        cost_estimate=pl.CostEstimate(
            flops=4 * rows * rows * cols * len(groups),
            bytes_accessed=8 * rows * cols,
            transcendentals=rows * rows * len(groups),
        ),
        name="attend",
    )(place, neighbours, tile_slot, *queries, *flat, *extra)


def finish_body(parts, *refs):
    out = refs[-1]
    total = None
    for key in range(parts):
        term = jnp.dot(
            refs[key][...], refs[parts + key][...], preferred_element_type=jnp.float32
        )
        total = term if total is None else total + term
    out[...] = total.astype(jnp.bfloat16)


def finish(pieces, weights, tile, tiles, held):
    length = pieces[0].shape[0]
    width = weights[0].shape[1]
    parts = len(pieces)
    extra = [] if held is None else [held]
    return pl.pallas_call(
        functools.partial(finish_body, parts),
        out_shape=jax.ShapeDtypeStruct((tiles * length, width), jnp.bfloat16),
        grid=(1,),
        in_specs=[pl.BlockSpec(p.shape, lambda i: (0, 0)) for p in pieces]
        + [pl.BlockSpec(w.shape, lambda i: (0, 0)) for w in weights]
        + [pl.BlockSpec(memory_space=pl.ANY)] * len(extra),
        out_specs=pl.BlockSpec((length, width), lambda i: (tile, 0)),
        input_output_aliases={2 * parts: 0} if extra else {},
        compiler_params=params(16),
        cost_estimate=pl.CostEstimate(
            flops=2 * length * pieces[0].shape[1] * parts * width,
            bytes_accessed=2 * length * width,
            transcendentals=0,
        ),
        name="finish",
    )(*pieces, *weights, *extra)


def turned(blocks, amount):
    count = lax.axis_size("tm")
    pairs = [(i, (i + amount) % count) for i in range(count)]
    return [lax.ppermute(block, "tm", pairs) for block in blocks]


def rest(amount, blocks, weights):
    if amount:
        blocks = turned(blocks, amount)
    out = None
    wide = [gathered(block) for block in blocks]
    for tile, pieces in enumerate(wide):
        out = finish(pieces, weights, tile, len(blocks), out)
    return out


def handed(blocks, weights, rotation):
    count = lax.axis_size("tm")
    stride = 1
    while stride * RADIX < count:
        digit = rotation // stride % RADIX
        branches = [lambda b: list(b)] + [
            functools.partial(turned, amount=d * stride) for d in range(1, RADIX)
        ]
        blocks = lax.switch(digit, branches, blocks)
        stride *= RADIX
    lowest = 1 if stride == 1 else 0
    digits = range(lowest, -(-count // stride))
    branches = [functools.partial(rest, d * stride) for d in digits]
    return lax.switch(rotation // stride - lowest, branches, blocks, weights)


def per_device(
    latents, w_query, w_key, w_value, q_gain, k_gain, w_out, neighbours, tile_slot, slab_dest
):
    rows = latents.shape[0]
    tiles = neighbours.shape[0]
    length = rows // tiles
    small = length // 3
    sizes = [length - small, small] * tiles
    me = lax.axis_index("head")
    place = jnp.stack([lax.axis_index("tm"), me]).astype(jnp.int32)
    gains = (q_gain.reshape(1, -1), k_gain.reshape(1, -1))

    queries, own, partner, other = [], [], [], []
    low = 0
    pieces = []
    for size in sizes:
        pieces.append(gathered(lax.slice_in_dim(latents, low, low + size, axis=0)))
        low += size
    for piece in pieces:
        q, kv = project(place, piece, w_query, w_key, w_value, *gains)
        queries.append(q)
        own.append(kv)
        partner.append(exchanged(kv))
        other.append(relayed(partner[-1]))

    heads = lax.axis_size("head")
    width = w_out.shape[1] // heads
    weights = []
    for key in range(heads):
        block = lax.dynamic_slice_in_dim(w_out, (me ^ key) * width, width, axis=1)
        if key:
            block, _ = lax.optimization_barrier((block, pieces[-1][-1]))
            block = flipped(block, key)
        weights.append(block)

    state = attend(place, neighbours, tile_slot, queries, [own, partner], ("own", "partner"), None)
    blocks = attend(place, neighbours, tile_slot, queries, [other], ("other",), state)
    return handed(list(blocks), weights, slab_dest[0])


def solution(mesh):
    return jax.shard_map(
        per_device,
        mesh=mesh,
        in_specs=(
            P("tm", "head"),
            P(None, "head"),
            P(None, "head"),
            P(None, "head"),
            P(),
            P(),
            P("head", None),
            P("tm", None),
            P(),
            P(),
        ),
        out_specs=P("tm", "head"),
        check_vma=False,
    )
```
